1024 devices in a mesh: pipe: 16 (over x, y_hi, core), expert: 64 (over z, y_lo).
Axes of the slice: x: 4, y: 4 (y_hi: 2, y_lo: 2; y = y_hi * 2 + y_lo), z: 32, core: 2. Of those that a mesh axis runs over, the one named last changes fastest.
Arguments:
- section_rows: bfloat16 [131072, 4096], P(('pipe', 'expert')), may hold values from -6 to 6
- route_ids: int32 [131072, 8], P(('pipe', 'expert')), may hold values from 0 to 127, as said below
- route_gates: bfloat16 [131072, 8], P(('pipe', 'expert')), may hold values from 0.099609375 to 1
- w_gate: bfloat16 [4096, 12288], P(None, 'expert'), may hold values from -0.09375 to 0.09375
- w_up: bfloat16 [4096, 12288], P(None, 'expert'), may hold values from -0.09375 to 0.09375
- w_down: bfloat16 [12288, 4096], P('expert'), may hold values from -0.15625 to 0.15625
Outputs:
- layer_out: bfloat16 [131072, 4096], P(('pipe', 'expert'))
The draws below stay inside these ranges and needn't reach their ends.
Inputs may be any that keep to these rules, and one draw needn't show every extreme that they name: `route_ids`: each row names 8 different experts. In the rows of one device at most 4 name any one expert below 8, and on every relay rank one such expert is named by exactly 4 rows of every device.
All inputs are finite; a program needn't handle non-finite values.
Results may differ from the reference program's by a relative error of at most 0.0026.
Values may be sent and summed in bfloat16 or wider, within the bound.
A program may use at most 32 MiB of HBM per device.

```python
import math
import jax
import jax.numpy as jnp
from jax import lax

D = 4096
FF = 1536
EXPERTS = 128
TOPK = 8
TOK_DEV = 128
GROUP = 8
CAP = 4
E_WIN = 8
TOKENS = 131072
N_EXPERT = 64


def draw_route_ids(key, part):
    base = jax.random.fold_in(key, 7)
    keys = jax.random.split(base, 5)
    blocks = TOKENS // TOK_DEV
    ranks = blocks // (E_WIN * GROUP)
    span = (EXPERTS - E_WIN) // TOPK
    hottest = jax.random.randint(keys[0], (ranks,), 0, E_WIN)
    counts = jax.random.randint(keys[1], (blocks, E_WIN), 0, CAP + 1)
    rank_of = jnp.arange(blocks) // (E_WIN * GROUP)
    counts = jnp.where(jnp.arange(E_WIN)[None, :] == hottest[rank_of][:, None], CAP, counts)
    scores = jax.random.randint(keys[2], (blocks, E_WIN, TOK_DEV), 0, 1 << 20) * TOK_DEV + jnp.arange(TOK_DEV)
    order = jnp.argsort(scores, axis=-1)
    placed = jnp.argsort(order, axis=-1)
    chosen = placed < counts[:, :, None]
    chosen = jnp.transpose(chosen, (0, 2, 1)).reshape(blocks * TOK_DEV, E_WIN)
    slots = jnp.arange(TOPK)
    others = E_WIN + slots[None, :] * span + jax.random.randint(keys[3], (blocks * TOK_DEV, TOPK), 0, span)
    window = jnp.concatenate([chosen, jnp.zeros((blocks * TOK_DEV, TOPK - E_WIN), bool)], axis=1)
    named = jnp.where(window, slots[None, :], others)
    mixing = jnp.argsort(jax.random.randint(keys[4], (blocks * TOK_DEV, TOPK), 0, 1 << 20) * TOPK + slots[None, :], axis=-1)
    return jnp.take_along_axis(named, mixing, axis=1).astype(jnp.int32)


def level_of(own_key, shape, shards, smallest, top_value):
    level, own = 1.0, jax.random.fold_in(own_key, 6)
    for dim, shards_of in shards:
        draws = jnp.exp(jax.random.uniform(jax.random.fold_in(own, dim), (shards_of,), jnp.float32, smallest / len(shards), top_value / len(shards)))
        level = level * jnp.repeat(draws, shape[dim] // shards_of).reshape([-1 if axis == dim else 1 for axis in range(len(shape))])
    return level


def bell_draw(own_key, shape, deviation, limit, cuts=(), held_as=jnp.bfloat16):
    factor_of = level_of(own_key, shape, cuts, -0.22, 0.18) if cuts else 1.0
    values = jax.random.normal(own_key, shape, jnp.float32) * deviation * factor_of
    return jnp.minimum(jnp.maximum(values, -limit), limit).astype(held_as)


def setup_inputs(seed: int = 0) -> dict:
    key_list = jax.random.split(jax.random.key(seed), 7)
    return {
        "section_rows": bell_draw(key_list[0], (TOKENS, D), 1.0, 6.0, ((0, 1024),)),
        "route_ids": draw_route_ids(jax.random.fold_in(key_list[6], 71), 0),
        "route_gates": jnp.clip(jnp.exp(math.log(1.0) - 2.306499 * jax.random.uniform(key_list[2], (TOKENS, TOPK), jnp.float32) ** level_of(key_list[2], (TOKENS, TOPK), ((0, 1024),), -0.2, 0.2)), 0.099609375, 1.0).astype(jnp.bfloat16),
        "w_gate": bell_draw(key_list[3], (D, E_WIN * FF), D ** -0.5, 0.09375, ((1, 64),)),
        "w_up": bell_draw(key_list[4], (D, E_WIN * FF), D ** -0.5, 0.09375, ((1, 64),)),
        "w_down": bell_draw(key_list[5], (E_WIN * FF, D), FF ** -0.5, 0.15625, ((0, 64),)),
    }


def rank_layer(packed_args, w_gate, w_up, w_down):
    xr, ids, gates = packed_args
    e_win = N_EXPERT // GROUP
    width = FF // GROUP
    blocks = xr.shape[0] // TOK_DEV
    xb = xr.reshape(blocks, TOK_DEV, D)
    total = jnp.zeros((blocks, TOK_DEV, D), jnp.float32)
    for expert_id in range(e_win):
        match = ids == expert_id
        hit = jnp.any(match, axis=1).reshape(blocks, TOK_DEV)
        weight = jnp.sum(jnp.where(match, gates.astype(jnp.float32), 0.0), axis=1).reshape(blocks, TOK_DEV)
        place = jnp.cumsum(hit.astype(jnp.int32), axis=1) - 1
        onehot = (hit[:, None, :] & (place[:, None, :] == jnp.arange(CAP, dtype=jnp.int32)[None, :, None])).astype(jnp.float32)
        packed = jnp.einsum("bct,btd->bcd", onehot, xb.astype(jnp.float32)).astype(jnp.bfloat16).reshape(blocks * CAP, D)
        start = expert_id * FF
        gate = jnp.dot(packed, w_gate[:, start:start + FF], preferred_element_type=jnp.float32)
        upper = jnp.dot(packed, w_up[:, start:start + FF], preferred_element_type=jnp.float32)
        hidden = (jax.nn.silu(gate) * upper).astype(jnp.bfloat16)
        expert_out = jnp.zeros((blocks * CAP, D), jnp.float32)
        for run in range(GROUP):
            part = jnp.dot(hidden[:, run * width:(run + 1) * width], w_down[start + run * width:start + (run + 1) * width, :], preferred_element_type=jnp.float32)
            expert_out = expert_out + part.astype(jnp.bfloat16).astype(jnp.float32)
        expert_out = expert_out.reshape(blocks, CAP, D)
        weighted = onehot * weight[:, None, :]
        total = total + jnp.einsum("bct,bcd->btd", weighted, expert_out, precision=lax.Precision.HIGHEST)
    result = (xb.astype(jnp.float32) + total).astype(jnp.bfloat16)
    return result.reshape(blocks * TOK_DEV, D)


def reference(section_rows, route_ids, route_gates, w_gate, w_up, w_down):
    offset = TOK_DEV * N_EXPERT
    rows = jnp.roll(section_rows, offset, axis=0)
    ids = jnp.roll(route_ids, offset, axis=0)
    gates = jnp.roll(route_gates, offset, axis=0)
    ranks = rows.shape[0] // offset
    stacked = (rows.reshape(ranks, offset, D), ids.reshape(ranks, offset, TOPK), gates.reshape(ranks, offset, TOPK))
    outputs = lax.map(lambda item: rank_layer(item, w_gate, w_up, w_down), stacked)
    return outputs.reshape(ranks * offset, D)
```

```python
import jax
import jax.numpy as jnp
from jax import lax
from jax.sharding import PartitionSpec as P

GROUP = 8
CAP = 4


def to_next(block, axis):
    n = lax.axis_size(axis)
    return lax.ppermute(block, axis, [(i, (i + 1) % n) for i in range(n)])


def routing(ids, gates, e_win):
    match = ids[:, :, None] == jnp.arange(e_win, dtype=jnp.int32)[None, None, :]
    hit = jnp.any(match, axis=1)
    weight = jnp.sum(jnp.where(match, gates.astype(jnp.float32)[:, :, None], 0.0), axis=1)
    place = jnp.cumsum(hit.astype(jnp.int32), axis=0) - 1
    slotted = hit[:, :, None] & (place[:, :, None] == jnp.arange(CAP, dtype=jnp.int32)[None, None, :])
    return slotted.reshape(ids.shape[0], e_win * CAP), weight


def local(section_rows, route_ids, route_gates, w_gate, w_up, w_down):
    devices = lax.axis_size("expert")
    e_win = devices // GROUP
    width = section_rows.shape[1]
    groups = [[g * GROUP + k for k in range(GROUP)] for g in range(e_win)]
    rows = to_next(section_rows, "pipe")
    slotted, weight = routing(route_ids, route_gates, e_win)
    packed = jnp.dot(slotted.astype(jnp.bfloat16).T, section_rows, preferred_element_type=jnp.float32).astype(jnp.bfloat16)
    half = CAP * width // GROUP
    outgoing = packed.reshape(e_win * GROUP, half)
    received = lax.all_to_all(outgoing, "expert", split_axis=0, concat_axis=0, tiled=True)
    gathered = lax.all_gather(received, "expert", axis_index_groups=groups, axis=0, tiled=False)
    flat = gathered.reshape(CAP, 2, devices, half).transpose(0, 2, 1, 3).reshape(CAP * devices, width)
    gate = jnp.dot(flat, w_gate, preferred_element_type=jnp.float32)
    upper = jnp.dot(flat, w_up, preferred_element_type=jnp.float32)
    hidden = (jax.nn.silu(gate) * upper).astype(jnp.bfloat16)
    partial_out = jnp.dot(hidden, w_down, preferred_element_type=jnp.float32).astype(jnp.bfloat16)
    pieces = partial_out.reshape(CAP, devices, 2, half).transpose(0, 2, 1, 3).reshape(GROUP, devices * half)
    spread = lax.all_to_all(pieces, "expert", split_axis=0, concat_axis=0, axis_index_groups=groups, tiled=True)
    summed = jnp.sum(spread.astype(jnp.float32), axis=0).astype(jnp.bfloat16).reshape(devices, half)
    returned = lax.all_to_all(summed, "expert", split_axis=0, concat_axis=0, tiled=True)
    returned = to_next(returned.reshape(e_win * CAP, width), "pipe")
    weighted = (slotted.astype(jnp.float32) * jnp.repeat(weight, CAP, axis=1)).astype(jnp.bfloat16)
    weighted = to_next(weighted, "pipe")
    mixed = jnp.dot(weighted, returned, preferred_element_type=jnp.float32)
    return (rows.astype(jnp.float32) + mixed).astype(jnp.bfloat16)


def solution(mesh):
    in_specs = (
        P(("pipe", "expert"), None),
        P(("pipe", "expert"), None),
        P(("pipe", "expert"), None),
        P(None, "expert"),
        P(None, "expert"),
        P("expert", None),
    )
    out_specs = P(("pipe", "expert"), None)
    return jax.shard_map(local, mesh=mesh, in_specs=in_specs, out_specs=out_specs, check_vma=False)
```
